32 devices in a mesh: group: 2 (over x), surf: 16 (over z, y, core).
Axes of the slice: x: 2, y: 2, z: 4, core: 2. Of those that a mesh axis runs over, the one named last changes fastest.
Arguments:
- traces: bfloat16 [4096, 128, 1024], P('surf', 'group'), parts along dimension 1, may hold values from -6 to 6
- operator: bfloat16 [4096, 8, 2, 4096], P('surf'), may hold values from -1 to 1, as said below
- freq_bins: int32 [8], replicated, may hold values from 1 to 511, as said below
- win_lengths: int32 [16], replicated, may hold values from 1 to 96, 1024 in all
- coefficients: float32 [16, 31], replicated, may hold values from -2.5 to 2.5
- neighbour: int32 [4096], P('surf'), may hold values from -2 to 2, as said below
Outputs:
- demultiple: bfloat16 [4096, 128, 1024], P('surf', 'group'), parts along dimension 1
The draws below stay inside these ranges and needn't reach their ends.
There are 2 independent parts, one for each index of `group`. The reference program is written for one: setup_inputs(seed, part) draws one part's arguments, and reference() takes and returns one part's arrays. A program takes and returns all parts, laid end to end along the dimension named above; an argument that names none is the same for every part. Nothing has to cross between parts.
Inputs may be any that keep to these rules, and one draw needn't show every extreme that they name: operator[i, f, c, j] equals operator[j, f, c, i] (reciprocity). `freq_bins`: the 8 bins are distinct. `neighbour`: points of even index take an offset of -2 or -1, points of odd index 1 or 2.
All inputs are finite; a program needn't handle non-finite values.
Results may differ from the reference program's by a relative error of at most 0.004.
Values may be sent and summed in bfloat16 or wider, within the bound.
A program may use at most 192 MiB of HBM per device.

```python
import math
import jax
import jax.numpy as jnp
import numpy as np
from jax import lax

NPTS = 4096
F = 8
NT = 1024
SHOTS = 64
TAPS = 31
HALO = 2
NWIN = 16


def draw_operator(key, part):
    values = jax.random.uniform(key, (NPTS, F, 2, NPTS), jnp.float32, -1.0, 1.0)
    mirrored = 0.5 * (values + jnp.transpose(values, (3, 1, 2, 0)))
    return (mirrored * (3.0 / NPTS) ** 0.5).astype(jnp.bfloat16)


def draw_freq_bins(key, part):
    return (jax.random.permutation(key, NT // 2 - 1)[:F] + 1).astype(jnp.int32)


def draw_neighbour(key, part):
    reach = jax.random.randint(key, (NPTS,), 1, 3, jnp.int32)
    parity = jnp.arange(NPTS, dtype=jnp.int32) % 2
    return (reach * (2 * parity - 1)).astype(jnp.int32)


def level_of(stream_key, shape, split, smallest, top_value):
    loudness = 1.0
    for dim, blocks in split:
        heights = jax.random.uniform(jax.random.fold_in(jax.random.fold_in(stream_key, 6), dim), (blocks,), jnp.float32, smallest / len(split), top_value / len(split))
        loudness = loudness * jnp.repeat(jnp.exp(heights), shape[dim] // blocks).reshape((-1,) + (1,) * (len(shape) - 1 - dim))
    return loudness


def profile(count, total, most, slope):
    portions = [(1 << 20) // math.isqrt(grade ** slope) + 1 for grade in range(2, count + 1)]
    rest, given = total - most - (count - 1), [1] * (count - 1)
    while rest > 0:
        movable = [i for i in range(count - 1) if given[i] < most]
        pool, left = sum([portions[i] for i in movable]), rest
        for i in movable:
            more = min(most - given[i], max(1, left * portions[i] // pool), rest)
            given[i] = given[i] + more
            rest = rest - more
    return np.array([most] + given)


def ragged(rng, amount, total, most, slope):
    if amount == 2:
        one = jax.random.randint(rng, (), max(1, total - most), min(most, total - 1) + 1)
        return jnp.stack([one, total - one])
    tallies = jnp.asarray(profile(amount, total, most, slope), jnp.int32)
    twos = (amount - 1) // 2
    giver, taker = tallies[1:1 + 2 * twos:2], tallies[2:2 + 2 * twos:2]
    margin = jnp.minimum(giver - 1, most - taker)
    moved = jax.random.randint(jax.random.fold_in(rng, 1), (twos,), 0, 1 << 20) % (margin + 1)
    tallies = tallies.at[1:1 + 2 * twos:2].set(giver - moved).at[2:2 + 2 * twos:2].set(taker + moved)
    return tallies[jax.random.permutation(jax.random.fold_in(rng, 2), amount)]


def gaussian(own_key, shape, spread, bound, shards=(), kind=jnp.bfloat16):
    array = jax.random.normal(own_key, shape, jnp.float32) * spread
    if len(shards) > 0:
        array = level_of(own_key, shape, shards, -0.22, 0.18) * array
    return jnp.clip(array, min=-bound, max=bound).astype(kind)


def setup_inputs(seed: int = 0, part: int = 0) -> dict:
    splits = jax.random.split(jax.random.key(seed), 7)
    own_keys = jax.random.split(jax.random.fold_in(splits[6], part), 7)
    traces = gaussian(own_keys[0], (NPTS, SHOTS, NT), 1.0, 6.0, ((0, 16),))
    operator = draw_operator(jax.random.fold_in(splits[6], 71), part)
    freq_bins = draw_freq_bins(jax.random.fold_in(splits[6], 71), part)
    win_lengths = ragged(splits[3], NWIN, NT, NT * 3 // (2 * NWIN), 0).astype(jnp.int32)
    coefficients = gaussian(splits[4], (NWIN, TAPS), 0.18, 2.5, (), jnp.float32)
    neighbour = draw_neighbour(jax.random.fold_in(splits[6], 71), part)
    return dict(traces=traces, operator=operator, freq_bins=freq_bins, win_lengths=win_lengths, coefficients=coefficients, neighbour=neighbour)


def angle_grid(freq_bins):
    sample_index = jnp.arange(NT, dtype=jnp.int32)
    phases = (sample_index[:, None] * freq_bins[None, :]) % NT
    return (2.0 * math.pi / NT) * phases.astype(jnp.float32)


def matching(multiple_estimate, coefficients, win_lengths):
    half_taps = (TAPS - 1) // 2
    window_ends = jnp.cumsum(win_lengths)
    sample_index = jnp.arange(NT, dtype=jnp.int32)
    window = jnp.sum((window_ends[None, :] <= sample_index[:, None]).astype(jnp.int32), axis=1)
    membership = (window[:, None] == jnp.arange(NWIN, dtype=jnp.int32)[None, :]).astype(jnp.float32)
    per_sample = jnp.dot(membership, coefficients, precision=lax.Precision.HIGHEST)
    padded = jnp.pad(multiple_estimate, ((0, 0), (0, 0), (half_taps, half_taps)))
    summed = jnp.zeros_like(multiple_estimate)
    for lag_index in range(TAPS):
        summed = summed + per_sample[:, lag_index] * padded[:, :, lag_index:lag_index + NT]
    return summed


def reference(traces, operator, freq_bins, win_lengths, coefficients, neighbour):
    angles = angle_grid(freq_bins)
    forward = jnp.stack([jnp.cos(angles), -jnp.sin(angles)], axis=2).reshape(NT, 2 * F).astype(jnp.bfloat16)
    spectra = jnp.dot(traces.reshape(NPTS * SHOTS, NT), forward, preferred_element_type=jnp.float32).astype(jnp.bfloat16)
    spectra = spectra.reshape(NPTS, SHOTS, F, 2).transpose(0, 2, 3, 1)
    dims = (((0,), (0,)), ((), ()))
    frequency_slices = []
    for freq_index in range(F):
        op_real = operator[:, freq_index, 0, :]
        op_imag = operator[:, freq_index, 1, :]
        sp_real = spectra[:, freq_index, 0, :]
        spectrum_imaginary = spectra[:, freq_index, 1, :]
        real_part = lax.dot_general(op_real, sp_real, dims, preferred_element_type=jnp.float32) - lax.dot_general(op_imag, spectrum_imaginary, dims, preferred_element_type=jnp.float32)
        imag_part = lax.dot_general(op_real, spectrum_imaginary, dims, preferred_element_type=jnp.float32) + lax.dot_general(op_imag, sp_real, dims, preferred_element_type=jnp.float32)
        frequency_slices.append(jnp.stack([real_part, imag_part], axis=1))
    predicted_multiples = jnp.stack(frequency_slices, axis=1)
    norm_divisor = (2.0 * F * NT) ** -0.5
    inverse_transform = norm_divisor * jnp.stack([jnp.cos(angles.T), -jnp.sin(angles.T)], axis=1)
    multiple_estimate = jnp.einsum("izwj,zwn->ijn", predicted_multiples, inverse_transform, precision=lax.Precision.HIGHEST)
    blocks = multiple_estimate.reshape(NPTS // 256, 256, SHOTS, NT)
    filtered = lax.map(lambda span_rows: matching(span_rows, coefficients, win_lengths), blocks).reshape(NPTS, SHOTS, NT)
    padded = jnp.pad(filtered, ((HALO, HALO), (0, 0), (0, 0)))
    adapted = filtered
    for offset in range(-HALO, HALO + 1):
        selector = (neighbour == offset).astype(jnp.float32)[:, None, None]
        adapted = adapted + 0.5 * selector * padded[HALO + offset:HALO + offset + NPTS]
    return (traces.astype(jnp.float32) - adapted).astype(jnp.bfloat16)
```

```python
import functools
import math

import jax
import jax.numpy as jnp
from jax import lax
from jax.experimental import pallas as pl
from jax.experimental.pallas import tpu as pltpu
from jax.sharding import PartitionSpec as P

TAPS = 31
HALO = 2
VMEM_LIMIT = 60 * 1024 * 1024
NT_DIMS = (((1,), (1,)), ((), ()))
TN_DIMS = (((0,), (0,)), ((), ()))


def angle_grid(freq_bins, samples):
    sample_index = jnp.arange(samples, dtype=jnp.int32)
    phases = sample_index[:, None] * freq_bins[None, :] % samples
    return 2.0 * math.pi / samples * phases.astype(jnp.float32)


def matching(multiple_estimate, coefficients, win_lengths):
    samples = multiple_estimate.shape[1]
    half_taps = (TAPS - 1) // 2
    window_ends = jnp.cumsum(win_lengths)
    sample_index = jnp.arange(samples, dtype=jnp.int32)
    window = jnp.sum((window_ends[None, :] <= sample_index[:, None]).astype(jnp.int32), axis=1)
    membership = (
        window[None, :] == jnp.arange(coefficients.shape[0], dtype=jnp.int32)[:, None]
    ).astype(jnp.float32)
    per_sample = jnp.dot(coefficients.T, membership, precision=lax.Precision.HIGHEST)
    padded = jnp.pad(multiple_estimate, ((0, 0), (half_taps, half_taps)))
    summed = jnp.zeros_like(multiple_estimate)
    for lag_index in range(TAPS):
        summed = summed + per_sample[lag_index][None] * padded[:, lag_index : lag_index + samples]
    return summed


def swap_halves(x, half):
    return pltpu.roll(x, half, axis=1)


def forward_kernel(freq_count, shots, traces_ref, table_ref, out_ref, lines):
    points = out_ref.shape[1]
    lanes = 2 * shots
    spectra = lax.dot_general(
        table_ref[...], traces_ref[...], NT_DIMS, preferred_element_type=jnp.float32
    )
    low = lax.broadcasted_iota(jnp.int32, (freq_count, lanes), 1) < shots
    for pair in range(points // 2):
        cols = slice(pair * lanes, (pair + 1) * lanes)
        real, imag = spectra[:freq_count, cols], spectra[freq_count:, cols]
        first = jnp.where(low, real, swap_halves(imag, shots))
        second = jnp.where(low, swap_halves(real, shots), imag)
        at = 2 * pair * freq_count
        lines[at : at + freq_count, :] = first
        lines[at + freq_count : at + 2 * freq_count, :] = second
    for f in range(freq_count):
        out_ref[f] = lines[pl.ds(f, points, stride=freq_count), :].astype(out_ref.dtype)


def forward(traces2, table, freq_count, shots, points):
    rows, samples = traces2.shape
    local = rows // shots
    return pl.pallas_call(
        functools.partial(forward_kernel, freq_count, shots),
        out_shape=jax.ShapeDtypeStruct((freq_count, local, 2 * shots), jnp.bfloat16),
        grid=(local // points,),
        in_specs=[
            pl.BlockSpec((points * shots, samples), lambda i: (i, 0)),
            pl.BlockSpec((2 * freq_count, samples), lambda i: (0, 0)),
        ],
        out_specs=pl.BlockSpec((freq_count, points, 2 * shots), lambda i: (0, i, 0)),
        scratch_shapes=[pltpu.VMEM((points * freq_count, 2 * shots), jnp.float32)],
        compiler_params=pltpu.CompilerParams(
            vmem_limit_bytes=VMEM_LIMIT, dimension_semantics=("arbitrary",)
        ),
        cost_estimate=pl.CostEstimate(
            flops=4 * freq_count * rows * samples,
            bytes_accessed=2 * rows * samples,
            transcendentals=0,
        ),
    )(traces2, table)


def adapt_kernel(
    freq_count, shots, points,
    near_ref, operator_ref, edge_ref, spectra_ref, basis_ref, traces_ref, out_ref,
    predicted, lines, split_basis,
):
    step = pl.program_id(0)
    local = operator_ref.shape[2]
    lanes = 2 * shots
    terms = 2 * freq_count

    def combined(real_rows, imag_rows):
        sign = jnp.where(
            lax.broadcasted_iota(jnp.int32, real_rows.shape, 1) < shots, -1.0, 1.0
        )
        return real_rows + sign * swap_halves(imag_rows, shots)

    @pl.when(step == 0)
    def _():
        basis = basis_ref[...]
        high = basis.astype(jnp.bfloat16)
        split_basis[0:terms, :] = high
        split_basis[terms : 2 * terms, :] = high
        split_basis[2 * terms :, :] = (basis - high.astype(jnp.float32)).astype(jnp.bfloat16)

    @pl.when(step < freq_count)
    def _():
        spectra = spectra_ref[:, 0].reshape(-1, lanes)
        real = jnp.dot(operator_ref[0, 0], spectra, preferred_element_type=jnp.float32)
        imag = jnp.dot(operator_ref[0, 1], spectra, preferred_element_type=jnp.float32)
        predicted[step, 8 : 8 + local, :] = combined(real, imag)
        edge = jnp.dot(edge_ref[0], spectra, preferred_element_type=jnp.float32)
        predicted[step, 0:8, :] = combined(edge[0:8], edge[8:16])

    @pl.when(step == freq_count - 1)
    def _():
        for f in range(freq_count):
            mine = predicted[f, 8 : 8 + local, :]
            lines[pl.ds(HALO * freq_count + f, local, stride=freq_count), :] = mine
            for h in range(HALO):
                before = h * freq_count + f
                lines[before : before + 1, :] = predicted[f, h : h + 1, :]
                after = (HALO + local + h) * freq_count + f
                lines[after : after + 1, :] = predicted[f, HALO + h : HALO + h + 1, :]

    @pl.when(step >= freq_count)
    def _():
        start = (step - freq_count) * points
        low = lax.broadcasted_iota(jnp.int32, (freq_count, lanes), 1) < shots

        def mixed(point):
            own = pl.multiple_of((point + HALO) * freq_count, freq_count)
            other = pl.multiple_of((point + HALO + near_ref[point]) * freq_count, freq_count)
            return lines[pl.ds(own, freq_count), :] + 0.5 * lines[pl.ds(other, freq_count), :]

        group = 8
        for part in range(points // group):
            reals, imags = [], []
            for pair in range(group // 2):
                first = mixed(start + part * group + 2 * pair)
                second = mixed(start + part * group + 2 * pair + 1)
                reals.append(jnp.where(low, first, swap_halves(second, shots)))
                imags.append(jnp.where(low, swap_halves(first, shots), second))
            terms_by_row = jnp.concatenate(
                [jnp.concatenate(reals, axis=1), jnp.concatenate(imags, axis=1)], axis=0
            )
            high = terms_by_row.astype(jnp.bfloat16)
            rest = (terms_by_row - high.astype(jnp.float32)).astype(jnp.bfloat16)
            left = jnp.concatenate([high, rest, high], axis=0)
            adapted = lax.dot_general(
                left, split_basis[...], TN_DIMS, preferred_element_type=jnp.float32
            )
            rows = slice(part * group * shots, (part + 1) * group * shots)
            out_ref[rows, :] = (traces_ref[rows, :].astype(jnp.float32) - adapted).astype(
                out_ref.dtype
            )


def adapt(near, operator, edge, spectra, basis, traces2, shots, points):
    freq_count, _, local, sources = operator.shape
    rows, samples = traces2.shape
    parts = spectra.shape[0]
    block = points * shots

    def f_of(i):
        return jnp.minimum(i, freq_count - 1)

    def row_of(i):
        return jnp.maximum(i - freq_count, 0)

    return pl.pallas_call(
        functools.partial(adapt_kernel, freq_count, shots, points),
        out_shape=jax.ShapeDtypeStruct((rows, samples), jnp.bfloat16),
        grid=(freq_count + local // points,),
        in_specs=[
            pl.BlockSpec(memory_space=pltpu.SMEM),
            pl.BlockSpec((1, 2, local, sources), lambda i: (f_of(i), 0, 0, 0)),
            pl.BlockSpec((1, 16, sources), lambda i: (f_of(i), 0, 0)),
            pl.BlockSpec((parts, 1, local, 2 * shots), lambda i: (0, f_of(i), 0, 0)),
            pl.BlockSpec((2 * freq_count, samples), lambda i: (0, 0)),
            pl.BlockSpec((block, samples), lambda i: (row_of(i), 0)),
        ],
        out_specs=pl.BlockSpec((block, samples), lambda i: (row_of(i), 0)),
        scratch_shapes=[
            pltpu.VMEM((freq_count, local + 8, 2 * shots), jnp.float32),
            pltpu.VMEM(((local + 2 * HALO) * freq_count, 2 * shots), jnp.float32),
            pltpu.VMEM((6 * freq_count, samples), jnp.bfloat16),
        ],
        compiler_params=pltpu.CompilerParams(
            vmem_limit_bytes=VMEM_LIMIT, dimension_semantics=("arbitrary",)
        ),
    )(near, operator, edge, spectra, basis, traces2)


def on_device(traces, operator, freq_bins, win_lengths, coefficients, neighbour):
    local, shots, samples = traces.shape
    freq_count = freq_bins.shape[0]
    size = lax.axis_size("surf")
    points = 16
    up = [(i, i + 1) for i in range(size - 1)]
    down = [(j, i) for i, j in up]
    before = lax.ppermute(operator[local - HALO :], "surf", up)
    after = lax.ppermute(operator[:HALO], "surf", down)
    edge = jnp.concatenate([before, after], axis=0).transpose(1, 2, 0, 3)
    edge = jnp.pad(edge, ((0, 0), (0, 0), (0, 8 - 2 * HALO), (0, 0)))
    edge = edge.reshape(freq_count, 16, operator.shape[3])

    angles = angle_grid(freq_bins, samples)
    table = jnp.concatenate([jnp.cos(angles.T), -jnp.sin(angles.T)], axis=0)
    norm = (2.0 * freq_count * samples) ** (-0.5)
    basis = matching(norm * table, coefficients, win_lengths)

    traces2 = traces.reshape(local * shots, samples)
    spectra = forward(traces2, table.astype(jnp.bfloat16), freq_count, shots, points)
    gathered = lax.all_gather(spectra, "surf")
    by_freq = operator.transpose(1, 2, 0, 3)
    out = adapt(neighbour, by_freq, edge, gathered, basis, traces2, shots, points)
    return out.reshape(local, shots, samples)


def solution(mesh):
    return jax.shard_map(
        on_device,
        mesh=mesh,
        in_specs=(P("surf", "group", None), P("surf", None, None, None), P(), P(), P(), P("surf")),
        out_specs=P("surf", "group", None),
        check_vma=False,
    )
```

```python
import functools
import math

import jax
import jax.numpy as jnp
from jax import lax
from jax.experimental import pallas as pl
from jax.experimental.pallas import tpu as pltpu
from jax.sharding import PartitionSpec as P

TAPS = 31
HALO = 2
VMEM_LIMIT = 60 * 1024 * 1024
NT_DIMS = (((1,), (1,)), ((), ()))
TN_DIMS = (((0,), (0,)), ((), ()))


def angle_grid(freq_bins, samples):
    sample_index = jnp.arange(samples, dtype=jnp.int32)
    phases = sample_index[:, None] * freq_bins[None, :] % samples
    return 2.0 * math.pi / samples * phases.astype(jnp.float32)


def matching(multiple_estimate, coefficients, win_lengths):
    samples = multiple_estimate.shape[1]
    half_taps = (TAPS - 1) // 2
    window_ends = jnp.cumsum(win_lengths)
    sample_index = jnp.arange(samples, dtype=jnp.int32)
    window = jnp.sum((window_ends[None, :] <= sample_index[:, None]).astype(jnp.int32), axis=1)
    membership = (
        window[None, :] == jnp.arange(coefficients.shape[0], dtype=jnp.int32)[:, None]
    ).astype(jnp.float32)
    per_sample = jnp.dot(coefficients.T, membership, precision=lax.Precision.HIGHEST)
    padded = jnp.pad(multiple_estimate, ((0, 0), (half_taps, half_taps)))
    summed = jnp.zeros_like(multiple_estimate)
    for lag_index in range(TAPS):
        summed = summed + per_sample[lag_index][None] * padded[:, lag_index : lag_index + samples]
    return summed


def swap_halves(x, half):
    return pltpu.roll(x, half, axis=1)


def forward_kernel(freq_count, shots, traces_ref, table_ref, out_ref, lines):
    points = out_ref.shape[1]
    lanes = 2 * shots
    spectra = lax.dot_general(
        table_ref[...], traces_ref[...], NT_DIMS, preferred_element_type=jnp.float32
    )
    low = lax.broadcasted_iota(jnp.int32, (freq_count, lanes), 1) < shots
    for pair in range(points // 2):
        cols = slice(pair * lanes, (pair + 1) * lanes)
        real, imag = spectra[:freq_count, cols], spectra[freq_count:, cols]
        first = jnp.where(low, real, swap_halves(imag, shots))
        second = jnp.where(low, swap_halves(real, shots), imag)
        at = 2 * pair * freq_count
        lines[at : at + freq_count, :] = first
        lines[at + freq_count : at + 2 * freq_count, :] = second
    for f in range(freq_count):
        out_ref[f] = lines[pl.ds(f, points, stride=freq_count), :].astype(out_ref.dtype)


def forward(traces2, table, freq_count, shots, points, chunk, chunks):
    rows, samples = traces2.shape
    rows = rows // chunks
    local = rows // shots
    first = chunk * (local // points)
    return pl.pallas_call(
        functools.partial(forward_kernel, freq_count, shots),
        out_shape=jax.ShapeDtypeStruct((freq_count, local, 2 * shots), jnp.bfloat16),
        grid=(local // points,),
        in_specs=[
            pl.BlockSpec((points * shots, samples), lambda i: (first + i, 0)),
            pl.BlockSpec((2 * freq_count, samples), lambda i: (0, 0)),
        ],
        out_specs=pl.BlockSpec((freq_count, points, 2 * shots), lambda i: (0, i, 0)),
        scratch_shapes=[pltpu.VMEM((points * freq_count, 2 * shots), jnp.float32)],
        compiler_params=pltpu.CompilerParams(
            vmem_limit_bytes=VMEM_LIMIT, dimension_semantics=("arbitrary",)
        ),
        cost_estimate=pl.CostEstimate(
            flops=4 * freq_count * rows * samples,
            bytes_accessed=2 * rows * samples,
            transcendentals=0,
        ),
    )(traces2, table)


def combined(real_rows, imag_rows, shots):
    low = lax.broadcasted_iota(jnp.int32, real_rows.shape, 1) < shots
    return real_rows + jnp.where(low, -1.0, 1.0) * swap_halves(imag_rows, shots)


def products(operator_refs, edge_refs, spectra_ref, shots):
    spectra = spectra_ref[:, 0].reshape(-1, 2 * shots)
    planes = [
        jnp.concatenate([ref[0, part] for ref in operator_refs], axis=1) for part in range(2)
    ]
    planes.append(jnp.concatenate([ref[0] for ref in edge_refs], axis=1))
    real, imag, edge = [
        jnp.dot(plane, spectra, preferred_element_type=jnp.float32) for plane in planes
    ]
    return combined(real, imag, shots), combined(edge[0:8], edge[8:16], shots)


def partial_kernel(shots, pieces, *refs):
    operator_refs, edge_refs = refs[:pieces], refs[pieces : 2 * pieces]
    spectra_ref, out_ref = refs[2 * pieces :]
    local = operator_refs[0].shape[2]
    main, edge = products(operator_refs, edge_refs, spectra_ref, shots)
    out_ref[0, 8 : 8 + local, :] = main
    out_ref[0, 0:8, :] = edge


def source_specs(local, sources, parts, chunk, chunks, f_of):
    pieces = parts if chunks > 1 else 1
    width = sources // (pieces * chunks)

    def column(piece):
        return piece * chunks + chunk

    operator_specs = [
        pl.BlockSpec((1, 2, local, width), lambda i, c=column(p): (f_of(i), 0, 0, c))
        for p in range(pieces)
    ]
    edge_specs = [
        pl.BlockSpec((1, 16, width), lambda i, c=column(p): (f_of(i), 0, c))
        for p in range(pieces)
    ]
    return pieces, operator_specs, edge_specs


def partial_product(operator, edge, spectra, shots, chunk, chunks):
    freq_count, _, local, sources = operator.shape
    parts, _, mine, lanes = spectra.shape
    pieces, operator_specs, edge_specs = source_specs(
        local, sources, parts, chunk, chunks, lambda i: i
    )
    return pl.pallas_call(
        functools.partial(partial_kernel, shots, pieces),
        out_shape=jax.ShapeDtypeStruct((freq_count, local + 8, lanes), jnp.float32),
        grid=(freq_count,),
        in_specs=operator_specs
        + edge_specs
        + [pl.BlockSpec((parts, 1, mine, lanes), lambda i: (0, i, 0, 0))],
        out_specs=pl.BlockSpec((1, local + 8, lanes), lambda i: (i, 0, 0)),
        compiler_params=pltpu.CompilerParams(
            vmem_limit_bytes=VMEM_LIMIT, dimension_semantics=("arbitrary",)
        ),
        cost_estimate=pl.CostEstimate(
            flops=4 * freq_count * local * (sources // chunks) * lanes,
            bytes_accessed=4 * freq_count * local * (sources // chunks),
            transcendentals=0,
        ),
    )(*([operator] * pieces), *([edge] * pieces), spectra)


def adapt_kernel(freq_count, shots, points, pieces, partials, *refs):
    near_ref, operator_refs, edge_refs = refs[0], refs[1 : 1 + pieces], refs[1 + pieces : 1 + 2 * pieces]
    spectra_ref = refs[1 + 2 * pieces]
    partial_refs = refs[2 + 2 * pieces : 2 + 2 * pieces + partials]
    basis_ref, traces_ref, out_ref, predicted, lines, split_basis = refs[2 + 2 * pieces + partials :]
    step = pl.program_id(0)
    local = operator_refs[0].shape[2]
    lanes = 2 * shots
    terms = 2 * freq_count

    @pl.when(step == 0)
    def _():
        basis = basis_ref[...]
        high = basis.astype(jnp.bfloat16)
        split_basis[0:terms, :] = high
        split_basis[terms : 2 * terms, :] = high
        split_basis[2 * terms :, :] = (basis - high.astype(jnp.float32)).astype(jnp.bfloat16)

    @pl.when(step < freq_count)
    def _():
        main, edge = products(operator_refs, edge_refs, spectra_ref, shots)
        for ref in partial_refs:
            main = main + ref[0, 8 : 8 + local, :]
            edge = edge + ref[0, 0:8, :]
        predicted[step, 8 : 8 + local, :] = main
        predicted[step, 0:8, :] = edge

    @pl.when(step == freq_count - 1)
    def _():
        for f in range(freq_count):
            mine = predicted[f, 8 : 8 + local, :]
            lines[pl.ds(HALO * freq_count + f, local, stride=freq_count), :] = mine
            for h in range(HALO):
                before = h * freq_count + f
                lines[before : before + 1, :] = predicted[f, h : h + 1, :]
                after = (HALO + local + h) * freq_count + f
                lines[after : after + 1, :] = predicted[f, HALO + h : HALO + h + 1, :]

    @pl.when(step >= freq_count)
    def _():
        start = (step - freq_count) * points
        low = lax.broadcasted_iota(jnp.int32, (freq_count, lanes), 1) < shots

        def mixed(point):
            own = pl.multiple_of((point + HALO) * freq_count, freq_count)
            other = pl.multiple_of((point + HALO + near_ref[point]) * freq_count, freq_count)
            return lines[pl.ds(own, freq_count), :] + 0.5 * lines[pl.ds(other, freq_count), :]

        group = 8
        for part in range(points // group):
            reals, imags = [], []
            for pair in range(group // 2):
                first = mixed(start + part * group + 2 * pair)
                second = mixed(start + part * group + 2 * pair + 1)
                reals.append(jnp.where(low, first, swap_halves(second, shots)))
                imags.append(jnp.where(low, swap_halves(first, shots), second))
            terms_by_row = jnp.concatenate(
                [jnp.concatenate(reals, axis=1), jnp.concatenate(imags, axis=1)], axis=0
            )
            high = terms_by_row.astype(jnp.bfloat16)
            rest = (terms_by_row - high.astype(jnp.float32)).astype(jnp.bfloat16)
            left = jnp.concatenate([high, rest, high], axis=0)
            adapted = lax.dot_general(
                left, split_basis[...], TN_DIMS, preferred_element_type=jnp.float32
            )
            rows = slice(part * group * shots, (part + 1) * group * shots)
            out_ref[rows, :] = (traces_ref[rows, :].astype(jnp.float32) - adapted).astype(
                out_ref.dtype
            )


def adapt(near, operator, edge, spectra, partial, basis, traces2, shots, points, chunk, chunks):
    freq_count, _, local, sources = operator.shape
    rows, samples = traces2.shape
    parts, _, mine, lanes = spectra.shape
    block = points * shots

    def f_of(i):
        return jnp.minimum(i, freq_count - 1)

    def row_of(i):
        return jnp.maximum(i - freq_count, 0)

    pieces, operator_specs, edge_specs = source_specs(local, sources, parts, chunk, chunks, f_of)
    partial_specs = [
        pl.BlockSpec((1, local + 8, lanes), lambda i: (f_of(i), 0, 0)) for _ in partial
    ]
    return pl.pallas_call(
        functools.partial(adapt_kernel, freq_count, shots, points, pieces, len(partial)),
        out_shape=jax.ShapeDtypeStruct((rows, samples), jnp.bfloat16),
        grid=(freq_count + local // points,),
        in_specs=[pl.BlockSpec(memory_space=pltpu.SMEM)]
        + operator_specs
        + edge_specs
        + [pl.BlockSpec((parts, 1, mine, lanes), lambda i: (0, f_of(i), 0, 0))]
        + partial_specs
        + [
            pl.BlockSpec((2 * freq_count, samples), lambda i: (0, 0)),
            pl.BlockSpec((block, samples), lambda i: (row_of(i), 0)),
        ],
        out_specs=pl.BlockSpec((block, samples), lambda i: (row_of(i), 0)),
        scratch_shapes=[
            pltpu.VMEM((freq_count, local + 8, lanes), jnp.float32),
            pltpu.VMEM(((local + 2 * HALO) * freq_count, lanes), jnp.float32),
            pltpu.VMEM((6 * freq_count, samples), jnp.bfloat16),
        ],
        compiler_params=pltpu.CompilerParams(
            vmem_limit_bytes=VMEM_LIMIT, dimension_semantics=("arbitrary",)
        ),
    )(near, *([operator] * pieces), *([edge] * pieces), spectra, *partial, basis, traces2)


def on_device(traces, operator, freq_bins, win_lengths, coefficients, neighbour):
    local, shots, samples = traces.shape
    freq_count = freq_bins.shape[0]
    size = lax.axis_size("surf")
    points = 32
    up = [(i, i + 1) for i in range(size - 1)]
    down = [(j, i) for i, j in up]
    before = lax.ppermute(operator[local - HALO :], "surf", up)
    after = lax.ppermute(operator[:HALO], "surf", down)
    edge = jnp.concatenate([before, after], axis=0).transpose(1, 2, 0, 3)
    edge = jnp.pad(edge, ((0, 0), (0, 0), (0, 8 - 2 * HALO), (0, 0)))
    edge = edge.reshape(freq_count, 16, operator.shape[3])

    angles = angle_grid(freq_bins, samples)
    table = jnp.concatenate([jnp.cos(angles.T), -jnp.sin(angles.T)], axis=0)
    norm = (2.0 * freq_count * samples) ** (-0.5)
    basis = matching(norm * table, coefficients, win_lengths)

    traces2 = traces.reshape(local * shots, samples)
    bf16_table = table.astype(jnp.bfloat16)
    chunks = 2 if local % 256 == 0 else 1
    gathered = []
    for chunk in range(chunks):
        spectra = forward(traces2, bf16_table, freq_count, shots, points, chunk, chunks)
        gathered.append(lax.all_gather(spectra, "surf"))
    by_freq = operator.transpose(1, 2, 0, 3)
    partial = []
    for chunk in range(chunks - 1):
        partial.append(partial_product(by_freq, edge, gathered[chunk], shots, chunk, chunks))
    out = adapt(
        neighbour, by_freq, edge, gathered[-1], partial, basis, traces2,
        shots, points, chunks - 1, chunks,
    )
    return out.reshape(local, shots, samples)


def solution(mesh):
    return jax.shard_map(
        on_device,
        mesh=mesh,
        in_specs=(P("surf", "group", None), P("surf", None, None, None), P(), P(), P(), P("surf")),
        out_specs=P("surf", "group", None),
        check_vma=False,
    )
```

```python
import functools
import math

import jax
import jax.numpy as jnp
from jax import lax
from jax.experimental import pallas as pl
from jax.experimental.pallas import tpu as pltpu
from jax.sharding import PartitionSpec as P

TAPS = 31
HALO = 2
VMEM_LIMIT = 60 * 1024 * 1024
NT_DIMS = (((1,), (1,)), ((), ()))
TN_DIMS = (((0,), (0,)), ((), ()))


def angle_grid(freq_bins, samples):
    sample_index = jnp.arange(samples, dtype=jnp.int32)
    phases = sample_index[:, None] * freq_bins[None, :] % samples
    return 2.0 * math.pi / samples * phases.astype(jnp.float32)


def matching(multiple_estimate, coefficients, win_lengths):
    samples = multiple_estimate.shape[1]
    half_taps = (TAPS - 1) // 2
    window_ends = jnp.cumsum(win_lengths)
    sample_index = jnp.arange(samples, dtype=jnp.int32)
    window = jnp.sum((window_ends[None, :] <= sample_index[:, None]).astype(jnp.int32), axis=1)
    membership = (
        window[None, :] == jnp.arange(coefficients.shape[0], dtype=jnp.int32)[:, None]
    ).astype(jnp.float32)
    per_sample = jnp.dot(coefficients.T, membership, precision=lax.Precision.HIGHEST)
    padded = jnp.pad(multiple_estimate, ((0, 0), (half_taps, half_taps)))
    summed = jnp.zeros_like(multiple_estimate)
    for lag_index in range(TAPS):
        summed = summed + per_sample[lag_index][None] * padded[:, lag_index : lag_index + samples]
    return summed


def swap_halves(x, half):
    return pltpu.roll(x, half, axis=1)


def forward_kernel(freq_count, shots, traces_ref, table_ref, out_ref, lines):
    points = out_ref.shape[1]
    lanes = 2 * shots
    spectra = lax.dot_general(
        table_ref[...], traces_ref[...], NT_DIMS, preferred_element_type=jnp.float32
    )
    low = lax.broadcasted_iota(jnp.int32, (freq_count, lanes), 1) < shots
    for pair in range(points // 2):
        cols = slice(pair * lanes, (pair + 1) * lanes)
        real, imag = spectra[:freq_count, cols], spectra[freq_count:, cols]
        first = jnp.where(low, real, swap_halves(imag, shots))
        second = jnp.where(low, swap_halves(real, shots), imag)
        at = 2 * pair * freq_count
        lines[at : at + freq_count, :] = first
        lines[at + freq_count : at + 2 * freq_count, :] = second
    for f in range(freq_count):
        out_ref[f] = lines[pl.ds(f, points, stride=freq_count), :].astype(out_ref.dtype)


def forward(traces2, table, freq_count, shots, points, chunk, chunks):
    rows, samples = traces2.shape
    rows = rows // chunks
    local = rows // shots
    first = chunk * (local // points)
    return pl.pallas_call(
        functools.partial(forward_kernel, freq_count, shots),
        out_shape=jax.ShapeDtypeStruct((freq_count, local, 2 * shots), jnp.bfloat16),
        grid=(local // points,),
        in_specs=[
            pl.BlockSpec((points * shots, samples), lambda i: (first + i, 0)),
            pl.BlockSpec((2 * freq_count, samples), lambda i: (0, 0)),
        ],
        out_specs=pl.BlockSpec((freq_count, points, 2 * shots), lambda i: (0, i, 0)),
        scratch_shapes=[pltpu.VMEM((points * freq_count, 2 * shots), jnp.float32)],
        compiler_params=pltpu.CompilerParams(
            vmem_limit_bytes=VMEM_LIMIT, dimension_semantics=("arbitrary",)
        ),
        cost_estimate=pl.CostEstimate(
            flops=4 * freq_count * rows * samples,
            bytes_accessed=2 * rows * samples,
            transcendentals=0,
        ),
    )(traces2, table)


def combined(real_rows, imag_rows, shots):
    low = lax.broadcasted_iota(jnp.int32, real_rows.shape, 1) < shots
    return real_rows + jnp.where(low, -1.0, 1.0) * swap_halves(imag_rows, shots)


def products(operator_refs, edge_refs, spectra_ref, shots):
    spectra = spectra_ref[:, 0].reshape(-1, 2 * shots)
    planes = [
        jnp.concatenate([ref[0, part] for ref in operator_refs], axis=1) for part in range(2)
    ]
    planes.append(jnp.concatenate([ref[0] for ref in edge_refs], axis=1))
    real, imag, edge = [
        jnp.dot(plane, spectra, preferred_element_type=jnp.float32) for plane in planes
    ]
    return combined(real, imag, shots), combined(edge[0:8], edge[8:16], shots)


def partial_kernel(shots, pieces, *refs):
    operator_refs, edge_refs = refs[:pieces], refs[pieces : 2 * pieces]
    spectra_ref, out_ref = refs[2 * pieces :]
    local = operator_refs[0].shape[2]
    main, edge = products(operator_refs, edge_refs, spectra_ref, shots)
    out_ref[0, 8 : 8 + local, :] = main
    out_ref[0, 0:8, :] = edge


def source_specs(local, sources, parts, chunk, chunks, f_of):
    pieces = parts if chunks > 1 else 1
    width = sources // (pieces * chunks)

    def column(piece):
        return piece * chunks + chunk

    operator_specs = [
        pl.BlockSpec((1, 2, local, width), lambda i, c=column(p): (f_of(i), 0, 0, c))
        for p in range(pieces)
    ]
    edge_specs = [
        pl.BlockSpec((1, 16, width), lambda i, c=column(p): (f_of(i), 0, c))
        for p in range(pieces)
    ]
    return pieces, operator_specs, edge_specs


def partial_product(operator, edge, spectra, shots, chunk, chunks):
    freq_count, _, local, sources = operator.shape
    parts, _, mine, lanes = spectra.shape
    pieces, operator_specs, edge_specs = source_specs(
        local, sources, parts, chunk, chunks, lambda i: i
    )
    return pl.pallas_call(
        functools.partial(partial_kernel, shots, pieces),
        out_shape=jax.ShapeDtypeStruct((freq_count, local + 8, lanes), jnp.float32),
        grid=(freq_count,),
        in_specs=operator_specs
        + edge_specs
        + [pl.BlockSpec((parts, 1, mine, lanes), lambda i: (0, i, 0, 0))],
        out_specs=pl.BlockSpec((1, local + 8, lanes), lambda i: (i, 0, 0)),
        compiler_params=pltpu.CompilerParams(
            vmem_limit_bytes=VMEM_LIMIT, dimension_semantics=("arbitrary",)
        ),
        cost_estimate=pl.CostEstimate(
            flops=4 * freq_count * local * (sources // chunks) * lanes,
            bytes_accessed=4 * freq_count * local * (sources // chunks),
            transcendentals=0,
        ),
    )(*([operator] * pieces), *([edge] * pieces), spectra)


def adapt_kernel(freq_count, shots, points, pieces, partials, *refs):
    near_ref, operator_refs, edge_refs = refs[0], refs[1 : 1 + pieces], refs[1 + pieces : 1 + 2 * pieces]
    spectra_ref = refs[1 + 2 * pieces]
    partial_refs = refs[2 + 2 * pieces : 2 + 2 * pieces + partials]
    basis_ref, traces_ref, out_ref, predicted, lines, split_basis = refs[2 + 2 * pieces + partials :]
    step = pl.program_id(0)
    local = operator_refs[0].shape[2]
    lanes = 2 * shots
    terms = 2 * freq_count

    @pl.when(step == 0)
    def _():
        basis = basis_ref[...]
        high = basis.astype(jnp.bfloat16)
        split_basis[0:terms, :] = high
        split_basis[terms : 2 * terms, :] = high
        split_basis[2 * terms :, :] = (basis - high.astype(jnp.float32)).astype(jnp.bfloat16)

    @pl.when(step < freq_count)
    def _():
        main, edge = products(operator_refs, edge_refs, spectra_ref, shots)
        for ref in partial_refs:
            main = main + ref[0, 8 : 8 + local, :]
            edge = edge + ref[0, 0:8, :]
        predicted[step, 8 : 8 + local, :] = main
        predicted[step, 0:8, :] = edge

    @pl.when(step == freq_count - 1)
    def _():
        for f in range(freq_count):
            mine = predicted[f, 8 : 8 + local, :]
            lines[pl.ds(HALO * freq_count + f, local, stride=freq_count), :] = mine
            for h in range(HALO):
                before = h * freq_count + f
                lines[before : before + 1, :] = predicted[f, h : h + 1, :]
                after = (HALO + local + h) * freq_count + f
                lines[after : after + 1, :] = predicted[f, HALO + h : HALO + h + 1, :]

    @pl.when(step >= freq_count)
    def _():
        start = (step - freq_count) * points
        low = lax.broadcasted_iota(jnp.int32, (freq_count, lanes), 1) < shots

        def mixed(point):
            own = pl.multiple_of((point + HALO) * freq_count, freq_count)
            other = pl.multiple_of((point + HALO + near_ref[point]) * freq_count, freq_count)
            return lines[pl.ds(own, freq_count), :] + 0.5 * lines[pl.ds(other, freq_count), :]

        group = 8
        for part in range(points // group):
            reals, imags = [], []
            for pair in range(group // 2):
                first = mixed(start + part * group + 2 * pair)
                second = mixed(start + part * group + 2 * pair + 1)
                reals.append(jnp.where(low, first, swap_halves(second, shots)))
                imags.append(jnp.where(low, swap_halves(first, shots), second))
            terms_by_row = jnp.concatenate(
                [jnp.concatenate(reals, axis=1), jnp.concatenate(imags, axis=1)], axis=0
            )
            high = terms_by_row.astype(jnp.bfloat16)
            rest = (terms_by_row - high.astype(jnp.float32)).astype(jnp.bfloat16)
            left = jnp.concatenate([high, rest, high], axis=0)
            adapted = lax.dot_general(
                left, split_basis[...], TN_DIMS, preferred_element_type=jnp.float32
            )
            rows = slice(part * group * shots, (part + 1) * group * shots)
            out_ref[rows, :] = (traces_ref[rows, :].astype(jnp.float32) - adapted).astype(
                out_ref.dtype
            )


def adapt(near, operator, edge, spectra, partial, basis, traces2, shots, points, chunk, chunks):
    freq_count, _, local, sources = operator.shape
    rows, samples = traces2.shape
    parts, _, mine, lanes = spectra.shape
    block = points * shots

    def f_of(i):
        return jnp.minimum(i, freq_count - 1)

    def row_of(i):
        return jnp.maximum(i - freq_count, 0)

    pieces, operator_specs, edge_specs = source_specs(local, sources, parts, chunk, chunks, f_of)
    partial_specs = [
        pl.BlockSpec((1, local + 8, lanes), lambda i: (f_of(i), 0, 0)) for _ in partial
    ]
    return pl.pallas_call(
        functools.partial(adapt_kernel, freq_count, shots, points, pieces, len(partial)),
        out_shape=jax.ShapeDtypeStruct((rows, samples), jnp.bfloat16),
        grid=(freq_count + local // points,),
        in_specs=[pl.BlockSpec(memory_space=pltpu.SMEM)]
        + operator_specs
        + edge_specs
        + [pl.BlockSpec((parts, 1, mine, lanes), lambda i: (0, f_of(i), 0, 0))]
        + partial_specs
        + [
            pl.BlockSpec((2 * freq_count, samples), lambda i: (0, 0)),
            pl.BlockSpec((block, samples), lambda i: (row_of(i), 0)),
        ],
        out_specs=pl.BlockSpec((block, samples), lambda i: (row_of(i), 0)),
        scratch_shapes=[
            pltpu.VMEM((freq_count, local + 8, lanes), jnp.float32),
            pltpu.VMEM(((local + 2 * HALO) * freq_count, lanes), jnp.float32),
            pltpu.VMEM((6 * freq_count, samples), jnp.bfloat16),
        ],
        compiler_params=pltpu.CompilerParams(
            vmem_limit_bytes=VMEM_LIMIT, dimension_semantics=("arbitrary",)
        ),
    )(near, *([operator] * pieces), *([edge] * pieces), spectra, *partial, basis, traces2)


def on_device(traces, operator, freq_bins, win_lengths, coefficients, neighbour):
    local, shots, samples = traces.shape
    freq_count = freq_bins.shape[0]
    size = lax.axis_size("surf")
    points = 32
    up = [(i, i + 1) for i in range(size - 1)]
    down = [(j, i) for i, j in up]
    before = lax.ppermute(operator[local - HALO :], "surf", up)
    after = lax.ppermute(operator[:HALO], "surf", down)
    edge = jnp.concatenate([before, after], axis=0).transpose(1, 2, 0, 3)
    edge = jnp.pad(edge, ((0, 0), (0, 0), (0, 8 - 2 * HALO), (0, 0)))
    edge = edge.reshape(freq_count, 16, operator.shape[3])

    angles = angle_grid(freq_bins, samples)
    table = jnp.concatenate([jnp.cos(angles.T), -jnp.sin(angles.T)], axis=0)
    norm = (2.0 * freq_count * samples) ** (-0.5)
    basis = matching(norm * table, coefficients, win_lengths)

    traces2 = traces.reshape(local * shots, samples)
    bf16_table = table.astype(jnp.bfloat16)
    chunks = 1
    gathered = []
    for chunk in range(chunks):
        spectra = forward(traces2, bf16_table, freq_count, shots, points, chunk, chunks)
        gathered.append(lax.all_gather(spectra, "surf"))
    by_freq = operator.transpose(1, 2, 0, 3)
    partial = []
    for chunk in range(chunks - 1):
        partial.append(partial_product(by_freq, edge, gathered[chunk], shots, chunk, chunks))
    out = adapt(
        neighbour, by_freq, edge, gathered[-1], partial, basis, traces2,
        shots, points, chunks - 1, chunks,
    )
    return out.reshape(local, shots, samples)


def solution(mesh):
    return jax.shard_map(
        on_device,
        mesh=mesh,
        in_specs=(P("surf", "group", None), P("surf", None, None, None), P(), P(), P(), P("surf")),
        out_specs=P("surf", "group", None),
        check_vma=False,
    )
```
